32 devices in a mesh: freq: 4 (over y, core), stcol: 8 (over z, x).
Axes of the slice: x: 2, y: 2, z: 4, core: 2. Of those that a mesh axis runs over, the one named last changes fastest.
Arguments:
- visibilities: float32 [2, 4, 512, 1, 512], P(None, 'freq', 'stcol'), may hold values from -28.8 to 28.8
- positions: float32 [3, 1, 512], replicated, may hold values from -3 to 3
- source_lmn: float32 [3, 1024], replicated, may hold values from -0.5 to 0.5
- source_flux: float32 [1024], replicated, may hold values from 0.02 to 0.2
- cluster_map: int32 [1024], replicated, may hold values from 0 to 15, as said below
- station_order: int32 [512], replicated, may hold values from 0 to 511, each once
- penalty: float32 [16], replicated, may hold values from 9.8304 to 196.608
- offsets: float32 [2, 4, 16, 512], P(None, 'freq'), may hold values from -1.2 to 1.2
Outputs:
- gains: float32 [2, 4, 16, 512], P(None, 'freq', None, 'stcol')
- consensus: float32 [2, 4, 16, 512], P(None, 'freq', None, 'stcol')
The draws below stay inside these ranges and needn't reach their ends.
Inputs may be any that keep to these rules, and one draw needn't show every extreme that they name: `cluster_map`: each of the 16 directions is named by exactly 64 sources. `station_order`: every station stands exactly once.
All inputs are finite; a program needn't handle non-finite values.
Results may differ from the reference program's by a relative error of at most 0.00011.
Values sent between devices are 32-bit elements; how exact they have to be, the bound alone decides.
A program may use at most 64 MiB of HBM per device.

```python
import math
import jax
import jax.numpy as jnp
from jax import lax

STATIONS = 512
DIRS = 16
SRC_DIR = 64
TIMES = 1
ADMM = 2
PASSES = 2
CHANNELS = 4
SOURCES = 1024


def draw_cluster_map(key, part):
    labels = jnp.arange(DIRS * SRC_DIR, dtype=jnp.int32) // SRC_DIR
    return jax.random.permutation(jax.random.fold_in(key, 11), labels)


def steps_of(stream_key, dims, cuts, low, largest):
    def one(dim, parts):
        heights = jax.random.uniform(jax.random.fold_in(jax.random.fold_in(stream_key, 6), dim), (parts,), jnp.float32, low / len(cuts), largest / len(cuts))
        return jnp.repeat(jnp.exp(heights), dims[dim] // parts).reshape((-1,) + (1,) * (len(dims) - dim - 1))

    loudness = one(*cuts[0])
    for cut in cuts[1:]:
        loudness = loudness * one(*cut)
    return loudness


def bell_draw(rng, extent, spread, reach, cuts=(), held_as=jnp.bfloat16):
    drawn = spread * jax.random.normal(rng, extent, jnp.float32)
    if cuts:
        drawn = drawn * steps_of(rng, extent, cuts, -0.22, 0.18)
    return jnp.clip(drawn, -reach, reach).astype(held_as)


def setup_inputs(seed: int = 0) -> dict:
    arg_keys = jax.random.split(jax.random.key(seed), 9)
    visibilities = bell_draw(arg_keys[0], (2, CHANNELS, STATIONS, TIMES, STATIONS), (0.15 * (DIRS * SRC_DIR) ** 0.5), 28.8, ((1, 4), (2, 8)), jnp.float32)
    positions = bell_draw(arg_keys[1], (3, TIMES, STATIONS), 0.5, 3.0, (), jnp.float32)
    source_lmn = jnp.clip(jax.random.uniform(arg_keys[2], (3, SOURCES), jnp.float32, -0.5, 0.5), -0.5, 0.5)
    source_flux = jnp.clip(jnp.exp(jax.random.uniform(arg_keys[3], (SOURCES,), jnp.float32, math.log(0.02), math.log(0.2))), 0.02, 0.2)
    cluster_map = draw_cluster_map(jax.random.fold_in(arg_keys[8], 71), 0)
    station_order = jax.random.permutation(arg_keys[5], STATIONS).astype(jnp.int32)
    penalty = jnp.clip(jnp.exp(jax.random.uniform(arg_keys[6], (DIRS,), jnp.float32, math.log(9.8304), math.log(196.608))), 9.8304, 196.608)
    offsets = bell_draw(arg_keys[7], (2, CHANNELS, DIRS, STATIONS), 0.2, 1.2, ((1, 4),), jnp.float32)
    return {"visibilities": visibilities, "positions": positions, "source_lmn": source_lmn, "source_flux": source_flux, "cluster_map": cluster_map, "station_order": station_order, "penalty": penalty, "offsets": offsets}


HIGHEST = lax.Precision.HIGHEST

def frequencies(channels):
    return 1.0 + 0.5 * jnp.arange(channels, dtype=jnp.float32) / channels

def basis_table(channels):
    centre = (jnp.arange(channels, dtype=jnp.float32) - 0.5 * (channels - 1)) / channels
    columns = [jnp.ones_like(centre), centre, centre * centre]
    finished = []
    for column in columns:
        for before in finished:
            column = column - jnp.sum(column * before) * before
        finished.append(column / jnp.sqrt(jnp.sum(column * column)))
    return jnp.stack(finished, axis=1)

def group_sources(source_lmn, source_flux, cluster_map, directions):
    ranking = jnp.argsort(cluster_map, stable=True)
    cosines = jnp.take(source_lmn, ranking, axis=1).reshape(3, directions, -1)
    brightness = jnp.take(source_flux, ranking).reshape(directions, -1)
    return (jnp.moveaxis(cosines, 1, 0), brightness)

def contract(row_part, column_part):
    return jnp.einsum('ctps,ctjs->cjtp', row_part, column_part, precision=HIGHEST)

def model_block(positions, direction_cosines, weights, freq_scale, column_ids):
    projected = positions[0][:, :, None] * direction_cosines[0] + positions[1][:, :, None] * direction_cosines[1]
    projected = projected + positions[2][:, :, None] * direction_cosines[2]
    phases = 2.0 * math.pi * freq_scale[:, None, None, None] * projected[None]
    cosine = jnp.cos(phases)
    sine_part = jnp.sin(phases)
    weighted_cos = cosine * weights
    weighted_sin = sine_part * weights
    column_cos = jnp.take(cosine, column_ids, axis=2)
    column_sin = jnp.take(sine_part, column_ids, axis=2)
    model_real = contract(weighted_cos, column_cos) + contract(weighted_sin, column_sin)
    model_imag = contract(weighted_sin, column_cos) - contract(weighted_cos, column_sin)
    station_ids = jnp.arange(positions.shape[2], dtype=jnp.int32)
    retained = (column_ids[:, None] != station_ids[None, :]).astype(model_real.dtype)
    retained = retained[None, :, None, :]
    return (model_real * retained, model_imag * retained)

def gain_update(numerator, denominator, gains, consensus, multiplier, penalty):
    weight_pen = penalty[:, None]
    scaling = 1.0 / (denominator + weight_pen)
    fresh = (numerator + gains * denominator + weight_pen * (consensus - multiplier)) * scaling
    return 0.5 * (gains + fresh)

def polynomial_fit(values, basis):
    coefficients = jnp.einsum('fj,rfkp->rjkp', basis, values, precision=HIGHEST)
    return jnp.einsum('fj,rjkp->rfkp', basis, coefficients, precision=HIGHEST)

def pass_terms(vis_chan, gains, model_real, model_imag, column_ids):
    column_gains = jnp.take(gains, column_ids, axis=3)
    column_real = jnp.moveaxis(column_gains[0], 1, 0)[:, :, :, None, None]
    column_imag = jnp.moveaxis(column_gains[1], 1, 0)[:, :, :, None, None]
    row_real = jnp.moveaxis(gains[0], 1, 0)[:, :, None, None, :]
    row_imag = jnp.moveaxis(gains[1], 1, 0)[:, :, None, None, :]
    along_real = model_real * column_real + model_imag * column_imag
    along_imag = model_imag * column_real - model_real * column_imag
    pred_real = row_real * along_real - row_imag * along_imag
    pred_imag = row_real * along_imag + row_imag * along_real
    resid_real = vis_chan[0] - lax.optimization_barrier(jnp.sum(pred_real, axis=0))
    resid_imag = vis_chan[1] - lax.optimization_barrier(jnp.sum(pred_imag, axis=0))
    num_real = lax.optimization_barrier(jnp.sum(resid_real * along_real + resid_imag * along_imag, axis=(2, 3)))
    num_imag = lax.optimization_barrier(jnp.sum(resid_imag * along_real - resid_real * along_imag, axis=(2, 3)))
    denominator = lax.optimization_barrier(jnp.sum(along_real * along_real + along_imag * along_imag, axis=(2, 3)))
    numerator = jnp.moveaxis(jnp.stack([num_real, num_imag]), 1, 2)
    return (numerator, jnp.moveaxis(denominator, 0, 1)[None])

def reference(visibilities, positions, source_lmn, source_flux, cluster_map, station_order, penalty, offsets):
    channels = visibilities.shape[1]
    directions = penalty.shape[0]
    freq_all = frequencies(channels)
    basis = basis_table(channels)
    cosines, brightness = group_sources(source_lmn, source_flux, cluster_map, directions)
    gains = jnp.stack([1.0 + offsets[0], offsets[1]])
    consensus = gains
    multiplier = jnp.zeros_like(gains)
    for admm_step in range(ADMM):

        def channel_work(items):
            vis_chan, freq_chan, gain_chan, cons_chan, mult_chan = items
            vis_chan = vis_chan[:, None]
            gain_chan = gain_chan[:, None]
            cons_chan = cons_chan[:, None]
            mult_chan = mult_chan[:, None]

            def one_model(entry):
                return model_block(positions, entry[0], entry[1], freq_chan[None], station_order)
            model_real, model_imag = lax.map(one_model, (cosines, brightness))
            for sweep_index in range(PASSES):
                numerator, denominator = pass_terms(vis_chan, gain_chan, model_real, model_imag, station_order)
                gain_chan = gain_update(numerator, denominator, gain_chan, cons_chan, mult_chan, penalty)
            return gain_chan[:, 0]
        solved = lax.map(channel_work, (jnp.moveaxis(visibilities, 1, 0), freq_all, jnp.moveaxis(gains, 1, 0), jnp.moveaxis(consensus, 1, 0), jnp.moveaxis(multiplier, 1, 0)))
        gains = jnp.moveaxis(solved, 0, 1)
        consensus = polynomial_fit(gains + multiplier, basis)
        multiplier = multiplier + gains - consensus
    return (gains, consensus)
```

```python
import functools

import jax
import jax.numpy as jnp
import numpy as np
from jax import lax
from jax.experimental import pallas as pl
from jax.experimental.pallas import tpu as pltpu
from jax.sharding import PartitionSpec as P

ADMM = 2
PASSES = 2

F32 = jnp.float32
BF16 = jnp.bfloat16
MESH = pl.DeviceIdType.MESH

SIN_COEFS = (6.2831852802614145, -10.335420167015846, 5.1001550464297125, -1.1965825712423341, 0.15531532061178804)
COS_COEFS = (0.9999999997799043, -4.934802137078822, 4.0587091595560825, -1.335212003047854, 0.2349373138047365, -0.02439632433202294)


def basis_table(channels):
    centre = (np.arange(channels, dtype=np.float32) - np.float32(0.5 * (channels - 1))) / np.float32(
        channels
    )
    finished = []
    for column in [np.ones_like(centre), centre, centre * centre]:
        for before in finished:
            column = column - np.sum(column * before) * before
        finished.append(column / np.sqrt(np.sum(column * column)))
    return np.stack(finished, axis=1).astype(np.float32)


def poly(coefs, u):
    out = coefs[-1] * u + coefs[-2]
    for c in coefs[-3::-1]:
        out = out * u + c
    return out


def cos_sin_turns(turns):
    r = turns - jnp.round(turns)
    u = r * r
    s2 = r * poly(SIN_COEFS, u)
    c = poly(COS_COEFS, u)
    return 1.0 - 0.5 * (s2 * s2), s2 * c


def split2(x):
    hi = x.astype(BF16)
    lo = (x - hi.astype(F32)).astype(BF16)
    return hi, lo


def dot(a, b):
    return lax.dot_general(a, b, (((1,), (0,)), ((), ())), preferred_element_type=F32)


def kernel(
    sizes,
    vis_ref,
    pos_ref,
    lmn_ref,
    flux_ref,
    cmap_ref,
    order_ref,
    pen_ref,
    off_ref,
    gains_ref,
    cons_ref,
    vsend,
    vrecv,
    scol,
    model,
    vrow,
    zbuf,
    gcol,
    grow,
    nd,
    gbuf,
    fbuf,
    vs_sem,
    vr_sem,
    gs_sem,
    gr_sem,
    fs_sem,
    fr_sem,
):
    nf, ns, K, N, own, cols, S = sizes
    row = lax.axis_index("freq")
    me = lax.axis_index("stcol")
    total = K * S
    basis = basis_table(nf)

    def st_peer(i):
        return lax.rem(me + i, ns)

    def fr_peer(i):
        return lax.rem(row + i, nf)

    barrier = pltpu.get_barrier_semaphore()
    for i in range(1, ns):
        pl.semaphore_signal(barrier, inc=1, device_id={"stcol": st_peer(i)}, device_id_type=MESH)
    for i in range(1, nf):
        pl.semaphore_signal(barrier, inc=1, device_id={"freq": fr_peer(i)}, device_id_type=MESH)

    for d in range(ns):
        vsend[d] = jnp.concatenate(
            [vis_ref[0, :, d * own : (d + 1) * own], vis_ref[1, :, d * own : (d + 1) * own]], axis=1
        )
    vrecv[pl.ds(me, 1)] = vsend[pl.ds(me, 1)]
    pl.semaphore_wait(barrier, ns + nf - 2)

    vcopies = []
    for i in range(1, ns):
        peer = st_peer(i)
        copy = pltpu.make_async_remote_copy(
            src_ref=vsend.at[peer],
            dst_ref=vrecv.at[me],
            send_sem=vs_sem.at[i],
            recv_sem=vr_sem.at[i],
            device_id={"stcol": peer},
            device_id_type=MESH,
        )
        copy.start()
        vcopies.append(copy)

    def own_lanes(get):
        out = get(0)
        for d in range(1, ns):
            out = jnp.where(me == d, get(d), out)
        return out

    nu = 1.0 + 0.5 * row.astype(F32) / nf
    pos = pos_ref[...] * nu
    pos_own = own_lanes(lambda d: pos[:, d * own : (d + 1) * own])
    pos_own2 = jnp.concatenate([pos_own, pos_own], axis=1)
    lane2 = lax.broadcasted_iota(jnp.int32, (1, 2 * own), 1)
    quarter = jnp.where(lane2 >= own, 0.25, 0.0).astype(F32)
    g_re = own_lanes(lambda d: off_ref[0, :, d * own : (d + 1) * own]) + 1.0
    g_im = own_lanes(lambda d: off_ref[1, :, d * own : (d + 1) * own])

    key = cmap_ref[...].astype(F32) * total + lax.broadcasted_iota(jnp.int32, (1, total), 1).astype(F32)
    key_col = jnp.broadcast_to(key, (8, total)).T[:, 0:1]
    rank = jnp.zeros((1, total), F32)
    chunk = 128
    for b in range(0, total, chunk):
        less = jnp.where(key_col[b : b + chunk] < key, 1.0, 0.0)
        rank = rank + jnp.sum(less, axis=0, keepdims=True)
    attr = jnp.concatenate([lmn_ref[...], flux_ref[...]], axis=0)
    a_hi = attr.astype(BF16).astype(F32)
    a_mid = (attr - a_hi).astype(BF16).astype(F32)
    a_lo = attr - a_hi - a_mid
    stacked = jnp.concatenate([a_hi, a_mid, a_lo, jnp.zeros((116, total), F32)], axis=0)
    attr_t = stacked.T.astype(BF16)
    step = min(256, total)

    def sort_body(b, carry):
        slot = lax.broadcasted_iota(jnp.int32, (step, total), 0) + b * step
        pick = jnp.where(slot.astype(F32) == rank, 1.0, 0.0).astype(BF16)
        got = dot(pick, attr_t)
        scol[pl.ds(pl.multiple_of(b * step, step), step), :] = (
            got + pltpu.roll(got, 124, 1) + pltpu.roll(got, 120, 1)
        )
        return carry

    lax.fori_loop(0, total // step, sort_body, 0)

    diag_rows = lax.rem(lax.broadcasted_iota(jnp.int32, (2 * own, N), 0), own) + me * own
    diag = diag_rows == lax.broadcasted_iota(jnp.int32, (2 * own, N), 1)

    def model_body(k, carry):
        src = scol[pl.ds(pl.multiple_of(k * S, S), S), :]
        sl, sm, sn, w = src[:, 0:1], src[:, 1:2], src[:, 2:3], src[:, 3:4]
        t_all = sl * pos[0:1] + sm * pos[1:2] + sn * pos[2:3]
        c_all, s_all = cos_sin_turns(t_all)
        t_own = sl * pos_own2[0:1] + sm * pos_own2[1:2] + sn * pos_own2[2:3] - quarter
        c_own, s_own = cos_sin_turns(t_own)
        left = jnp.concatenate([c_own * w, s_own * w], axis=0).T
        l_hi, l_lo = split2(left)
        r_hi, r_lo = split2(jnp.concatenate([c_all, s_all], axis=0))
        m = dot(jnp.concatenate([l_hi, l_lo, l_hi], axis=1), jnp.concatenate([r_hi, r_hi, r_lo], axis=0))
        model[k] = jnp.where(diag, 0.0, m)
        return carry

    lax.fori_loop(0, K, model_body, 0)

    for copy in vcopies:
        copy.wait()
    place = lax.broadcasted_iota(jnp.int32, (N, N), 0) == order_ref[...]
    place = jnp.where(place, 1.0, 0.0).astype(BF16)
    v_hi, v_lo = split2(vrecv[...].reshape(N, 2 * own))
    got = dot(place, v_hi) + dot(place, v_lo)
    vrow[...] = got.T

    pen = pen_ref[...]
    lane = lax.broadcasted_iota(jnp.int32, (8, 128), 1)

    def set_rows(re, im):
        both = jnp.concatenate([re, im], axis=0)
        grow[:, : 2 * K] = both.T

    def terms():
        def body(i, carry):
            up = pl.ds(pl.multiple_of(8 * i, 8), 8)
            down = pl.ds(pl.multiple_of(own + 8 * i, 8), 8)
            res_r = vrow[up, :]
            res_i = vrow[down, :]
            row_g = grow[up, :]
            out = jnp.zeros((8, 128), F32)
            for k in range(K):
                mr = model[k, up, :]
                mi = model[k, down, :]
                cr = gcol[k : k + 1, :]
                ci = gcol[K + k : K + k + 1, :]
                zr = mr * cr + mi * ci
                zi = mi * cr - mr * ci
                zbuf[k, 0:8] = zr
                zbuf[k, 8:16] = zi
                rr = row_g[:, k : k + 1]
                ri = row_g[:, K + k : K + k + 1]
                res_r = res_r - (rr * zr - ri * zi)
                res_i = res_i - (rr * zi + ri * zr)
                dn = jnp.sum(zr * zr + zi * zi, axis=1, keepdims=True)
                out = jnp.where(lane == 2 * K + k, dn, out)
            for k in range(K):
                zr = zbuf[k, 0:8]
                zi = zbuf[k, 8:16]
                nr = jnp.sum(res_r * zr + res_i * zi, axis=1, keepdims=True)
                ni = jnp.sum(res_i * zr - res_r * zi, axis=1, keepdims=True)
                out = jnp.where(lane == k, nr, out)
                out = jnp.where(lane == K + k, ni, out)
            nd[up, :] = out
            return carry

        lax.fori_loop(0, own // 8, body, 0)
        flipped = nd[...].T
        return flipped[0:K], flipped[K : 2 * K], flipped[2 * K : 3 * K]

    def exchange(buf, stage, count, mine, name, peer_of, send_sem, recv_sem, block):
        buf[stage, pl.ds(mine, 1)] = block[None]
        copies = []
        for i in range(1, count):
            copy = pltpu.make_async_remote_copy(
                src_ref=buf.at[stage, mine],
                dst_ref=buf.at[stage, mine],
                send_sem=send_sem.at[stage, i],
                recv_sem=recv_sem.at[stage, i],
                device_id={name: peer_of(i)},
                device_id_type=MESH,
            )
            copy.start()
            copies.append(copy)
        return copies

    def fit(step, re, im):
        b_row = [
            functools.reduce(
                lambda acc, f: jnp.where(row == f, float(basis[f, j]), acc), range(1, nf), float(basis[0, j])
            )
            for j in range(3)
        ]
        out = None
        for j in range(3):
            coef = float(basis[0, j]) * fbuf[step, 0]
            for f in range(1, nf):
                coef = coef + float(basis[f, j]) * fbuf[step, f]
            part = b_row[j] * coef
            out = part if out is None else out + part
        return out[:, :own], out[:, own:]

    gcol[0:K, :] = off_ref[0] + 1.0
    gcol[K : 2 * K, :] = off_ref[1]
    grow[...] = jnp.zeros_like(grow)
    set_rows(g_re, g_im)
    c_re, c_im = g_re, g_im
    d_re = d_im = jnp.zeros_like(g_re)
    fit_copies = None
    stage = 0
    for admm in range(ADMM):
        for sweep in range(PASSES):
            nr, ni, dn = terms()
            if fit_copies is not None:
                for copy in fit_copies:
                    copy.wait()
                fit_copies = None
                c_re, c_im = fit(admm - 1, None, None)
                d_re = d_re + g_re - c_re
                d_im = d_im + g_im - c_im
            scaling = 1.0 / (dn + pen)
            f_re = (nr + g_re * dn + pen * (c_re - d_re)) * scaling
            f_im = (ni + g_im * dn + pen * (c_im - d_im)) * scaling
            g_re = 0.5 * (g_re + f_re)
            g_im = 0.5 * (g_im + f_im)
            last = admm == ADMM - 1 and sweep == PASSES - 1
            if not last:
                copies = exchange(
                    gbuf, stage, ns, me, "stcol", st_peer, gs_sem, gr_sem,
                    jnp.concatenate([g_re, g_im], axis=1),
                )
            if sweep == PASSES - 1:
                fit_copies = exchange(
                    fbuf, admm, nf, row, "freq", fr_peer, fs_sem, fr_sem,
                    jnp.concatenate([g_re + d_re, g_im + d_im], axis=1),
                )
            if not last:
                set_rows(g_re, g_im)
                for copy in copies:
                    copy.wait()
                gcol[0:K, :] = jnp.concatenate([gbuf[stage, d][:, :own] for d in range(ns)], axis=1)
                gcol[K : 2 * K, :] = jnp.concatenate([gbuf[stage, d][:, own:] for d in range(ns)], axis=1)
                stage += 1
    gains_ref[0] = g_re
    gains_ref[1] = g_im
    for copy in fit_copies:
        copy.wait()
    c_re, c_im = fit(ADMM - 1, None, None)
    cons_ref[0] = c_re
    cons_ref[1] = c_im


def on_device(
    visibilities, positions, source_lmn, source_flux, cluster_map, station_order, penalty, offsets
):
    nf = lax.axis_size("freq")
    ns = lax.axis_size("stcol")
    cols = visibilities.shape[2]
    N = visibilities.shape[4]
    K = penalty.shape[0]
    total = source_flux.shape[0]
    S = total // K
    own = N // ns
    assert visibilities.shape[1] == 1 and visibilities.shape[3] == 1
    exchanges = ADMM * PASSES - 1
    vmem = pl.BlockSpec(memory_space=pltpu.VMEM)
    shape = jax.ShapeDtypeStruct((2, K, own), F32)
    dma = pltpu.SemaphoreType.DMA
    gains, cons = pl.pallas_call(
        functools.partial(kernel, (nf, ns, K, N, own, cols, S)),
        out_shape=(shape, shape),
        in_specs=[vmem] * 8,
        out_specs=(vmem, vmem),
        scratch_shapes=[
            pltpu.VMEM((ns, cols, 2 * own), F32),
            pltpu.VMEM((ns, cols, 2 * own), F32),
            pltpu.VMEM((total, 128), F32),
            pltpu.VMEM((K, 2 * own, N), F32),
            pltpu.VMEM((2 * own, N), F32),
            pltpu.VMEM((K, 16, N), F32),
            pltpu.VMEM((2 * K, N), F32),
            pltpu.VMEM((own, 128), F32),
            pltpu.VMEM((own, 128), F32),
            pltpu.VMEM((exchanges, ns, K, 2 * own), F32),
            pltpu.VMEM((ADMM, nf, K, 2 * own), F32),
            dma((ns,)),
            dma((ns,)),
            dma((exchanges, ns)),
            dma((exchanges, ns)),
            dma((ADMM, nf)),
            dma((ADMM, nf)),
        ],
        compiler_params=pltpu.CompilerParams(collective_id=0, has_side_effects=True),
        name="calibrate",
    )(
        visibilities.reshape(2, cols, N),
        positions.reshape(3, N),
        source_lmn,
        source_flux.reshape(1, total),
        cluster_map.reshape(1, total),
        station_order.reshape(1, N),
        penalty.reshape(K, 1),
        offsets.reshape(2, K, N),
    )
    return gains[:, None], cons[:, None]


def solution(mesh):
    in_specs = (
        P(None, "freq", "stcol", None, None),
        P(),
        P(),
        P(),
        P(),
        P(),
        P(),
        P(None, "freq", None, None),
    )
    out_specs = (P(None, "freq", None, "stcol"), P(None, "freq", None, "stcol"))
    return jax.shard_map(
        on_device, mesh=mesh, in_specs=in_specs, out_specs=out_specs, check_vma=False
    )
```

```python
import functools

import jax
import jax.numpy as jnp
import numpy as np
from jax import lax
from jax.experimental import pallas as pl
from jax.experimental.pallas import tpu as pltpu
from jax.sharding import PartitionSpec as P

ADMM = 2
PASSES = 2

F32 = jnp.float32
BF16 = jnp.bfloat16
MESH = pl.DeviceIdType.MESH

SIN_COEFS = (4.442882919124344, -7.308245686509103, 3.6063542184332404, -0.8461116503750895, 0.10982451642675807)
COS_COEFS = (1.414213496255229, -6.978850948563844, 5.739460376907473, -1.883557905987641, 0.31068802752730623)


def basis_table(channels):
    centre = (np.arange(channels, dtype=np.float32) - np.float32(0.5 * (channels - 1))) / np.float32(
        channels
    )
    finished = []
    for column in [np.ones_like(centre), centre, centre * centre]:
        for before in finished:
            column = column - np.sum(column * before) * before
        finished.append(column / np.sqrt(np.sum(column * column)))
    return np.stack(finished, axis=1).astype(np.float32)


def poly(coefs, u):
    out = coefs[-1] * u + coefs[-2]
    for c in coefs[-3::-1]:
        out = out * u + c
    return out


def cos_sin_turns(turns):
    r = turns - jnp.round(turns)
    u = r * r
    s2 = r * poly(SIN_COEFS, u)
    c = poly(COS_COEFS, u)
    return 1.0 - s2 * s2, s2 * c


def split2(x):
    hi = x.astype(BF16)
    lo = (x - hi.astype(F32)).astype(BF16)
    return hi, lo


def dot(a, b):
    return lax.dot_general(a, b, (((1,), (0,)), ((), ())), preferred_element_type=F32)


def kernel(
    sizes,
    vis_ref,
    pos_ref,
    lmn_ref,
    flux_ref,
    cmap_ref,
    order_ref,
    pen_ref,
    off_ref,
    out_ref,
    vsend,
    vrecv,
    scol,
    model,
    vrow,
    zbuf,
    gcol,
    grow,
    nd,
    gbuf,
    fbuf,
    vs_sem,
    vr_sem,
    gs_sem,
    gr_sem,
    fs_sem,
    fr_sem,
):
    nf, ns, K, N, own, cols, S = sizes
    row = lax.axis_index("freq")
    me = lax.axis_index("stcol")
    total = K * S
    basis = basis_table(nf)

    def st_peer(i):
        return lax.rem(me + i, ns)

    def fr_peer(i):
        return lax.rem(row + i, nf)

    barrier = pltpu.get_barrier_semaphore()
    for i in range(1, ns):
        pl.semaphore_signal(barrier, inc=1, device_id={"stcol": st_peer(i)}, device_id_type=MESH)
    for i in range(1, nf):
        pl.semaphore_signal(barrier, inc=1, device_id={"freq": fr_peer(i)}, device_id_type=MESH)

    per = N // 128
    tiles = [
        [vis_ref[pl.ds(r * cols * per + t, cols, stride=per), :] for t in range(per)] for r in range(2)
    ]
    for d in range(ns):
        tile, at = divmod(d * own, 128)
        vsend[d] = jnp.concatenate([tiles[0][tile][:, at : at + own], tiles[1][tile][:, at : at + own]], axis=1)
    vrecv[pl.ds(me, 1)] = vsend[pl.ds(me, 1)]
    pl.semaphore_wait(barrier, ns + nf - 2)

    vcopies = []
    for i in range(1, ns):
        peer = st_peer(i)
        copy = pltpu.make_async_remote_copy(
            src_ref=vsend.at[peer],
            dst_ref=vrecv.at[me],
            send_sem=vs_sem.at[i],
            recv_sem=vr_sem.at[i],
            device_id={"stcol": peer},
            device_id_type=MESH,
        )
        copy.start()
        vcopies.append(copy)

    def own_lanes(get):
        out = get(0)
        for d in range(1, ns):
            out = jnp.where(me == d, get(d), out)
        return out

    nu = 1.0 + 0.5 * row.astype(F32) / nf
    pos = pos_ref[:, 0, :] * nu
    pos_own = own_lanes(lambda d: pos[:, d * own : (d + 1) * own])
    pos_own2 = jnp.concatenate([pos_own, pos_own], axis=1)
    lane2 = lax.broadcasted_iota(jnp.int32, (1, 2 * own), 1)
    quarter = jnp.where(lane2 >= own, 0.25, 0.0).astype(F32)
    g_re = own_lanes(lambda d: off_ref[0, :, d * own : (d + 1) * own]) + 1.0
    g_im = own_lanes(lambda d: off_ref[1, :, d * own : (d + 1) * own])

    cmap = cmap_ref[...]
    member = jnp.where(lax.broadcasted_iota(jnp.int32, (K, total), 0) == cmap, 1.0, 0.0)
    before = jnp.where(
        lax.broadcasted_iota(jnp.int32, (128, 128), 0) < lax.broadcasted_iota(jnp.int32, (128, 128), 1), 1.0, 0.0
    ).astype(BF16)
    seen = jnp.zeros((K, 1), F32)
    places = []
    for b in range(0, total, 128):
        part = member[:, b : b + 128]
        count = dot(part.astype(BF16), before) + seen
        places.append(jnp.sum(count * part, axis=0, keepdims=True))
        seen = seen + jnp.sum(part, axis=1, keepdims=True)
    place_row = jnp.concatenate(places, axis=1)
    pick = jnp.where(
        lax.broadcasted_iota(jnp.int32, (S, total), 0).astype(F32) == place_row, 1.0, 0.0
    ).astype(BF16)
    attr = jnp.concatenate([lmn_ref[...], flux_ref[...]], axis=0)
    a_hi = attr.astype(BF16).astype(F32)
    a_mid = (attr - a_hi).astype(BF16).astype(F32)
    a_lo = attr - a_hi - a_mid
    got = jnp.zeros((S, 128), F32)
    for part in (a_hi, a_mid, a_lo):
        spread = jnp.concatenate(
            [member * part[a : a + 1] for a in range(4)] + [jnp.zeros((128 - 4 * K, total), F32)], axis=0
        ).astype(BF16)
        got = got + lax.dot_general(
            pick, spread, (((1,), (1,)), ((), ())), preferred_element_type=F32
        )
    scol[...] = got

    diag_rows = lax.rem(lax.broadcasted_iota(jnp.int32, (2 * own, N), 0), own) + me * own
    diag = diag_rows == lax.broadcasted_iota(jnp.int32, (2 * own, N), 1)

    def model_body(k, carry):
        src = pltpu.roll(scol[...], 128 - k, 1)
        sl, sm, sn, w = (src[:, a * K : a * K + 1] for a in range(4))
        t_all = sl * pos[0:1] + sm * pos[1:2] + sn * pos[2:3]
        c_all, s_all = cos_sin_turns(t_all)
        t_own = sl * pos_own2[0:1] + sm * pos_own2[1:2] + sn * pos_own2[2:3] - quarter
        c_own, s_own = cos_sin_turns(t_own)
        left = jnp.concatenate([c_own * w, s_own * w], axis=0).T
        l_hi, l_lo = split2(left)
        r_hi, r_lo = split2(jnp.concatenate([c_all, s_all], axis=0))
        m = dot(jnp.concatenate([l_hi, l_lo, l_hi], axis=1), jnp.concatenate([r_hi, r_hi, r_lo], axis=0))
        model[k] = jnp.where(diag, 0.0, m)
        return carry

    lax.fori_loop(0, K, model_body, 0)

    for copy in vcopies:
        copy.wait()
    place = lax.broadcasted_iota(jnp.int32, (N, N), 0) == order_ref[...]
    place = jnp.where(place, 1.0, 0.0).astype(BF16)
    v_hi, v_lo = split2(vrecv[...].reshape(N, 2 * own))
    got = dot(place, v_hi) + dot(place, v_lo)
    vrow[...] = got.T

    pen = jnp.broadcast_to(pen_ref[...], (8, K)).T[:, 0:1]
    lane = lax.broadcasted_iota(jnp.int32, (8, 128), 1)

    def set_rows(re, im):
        both = jnp.concatenate([re, im], axis=0)
        grow[:, : 2 * K] = both.T

    def terms():
        def body(i, carry):
            up = pl.ds(pl.multiple_of(8 * i, 8), 8)
            down = pl.ds(pl.multiple_of(own + 8 * i, 8), 8)
            res_r = vrow[up, :]
            res_i = vrow[down, :]
            row_g = grow[up, :]
            out = jnp.zeros((8, 128), F32)
            for k in range(K):
                mr = model[k, up, :]
                mi = model[k, down, :]
                cr = gcol[k : k + 1, :]
                ci = gcol[K + k : K + k + 1, :]
                zr = mr * cr + mi * ci
                zi = mi * cr - mr * ci
                zbuf[k, 0:8] = zr
                zbuf[k, 8:16] = zi
                rr = row_g[:, k : k + 1]
                ri = row_g[:, K + k : K + k + 1]
                res_r = res_r - (rr * zr - ri * zi)
                res_i = res_i - (rr * zi + ri * zr)
                dn = jnp.sum(zr * zr + zi * zi, axis=1, keepdims=True)
                out = jnp.where(lane == 2 * K + k, dn, out)
            for k in range(K):
                zr = zbuf[k, 0:8]
                zi = zbuf[k, 8:16]
                nr = jnp.sum(res_r * zr + res_i * zi, axis=1, keepdims=True)
                ni = jnp.sum(res_i * zr - res_r * zi, axis=1, keepdims=True)
                out = jnp.where(lane == k, nr, out)
                out = jnp.where(lane == K + k, ni, out)
            nd[up, :] = out
            return carry

        lax.fori_loop(0, own // 8, body, 0)
        flipped = nd[...].T
        return flipped[0:K], flipped[K : 2 * K], flipped[2 * K : 3 * K]

    def exchange(buf, stage, count, mine, name, peer_of, send_sem, recv_sem, block):
        buf[stage, pl.ds(mine, 1)] = block[None]
        copies = []
        for i in range(1, count):
            copy = pltpu.make_async_remote_copy(
                src_ref=buf.at[stage, mine],
                dst_ref=buf.at[stage, mine],
                send_sem=send_sem.at[stage, i],
                recv_sem=recv_sem.at[stage, i],
                device_id={name: peer_of(i)},
                device_id_type=MESH,
            )
            copy.start()
            copies.append(copy)
        return copies

    def fit(step, re, im):
        b_row = [
            functools.reduce(
                lambda acc, f: jnp.where(row == f, float(basis[f, j]), acc), range(1, nf), float(basis[0, j])
            )
            for j in range(3)
        ]
        out = None
        for j in range(3):
            coef = float(basis[0, j]) * fbuf[step, 0]
            for f in range(1, nf):
                coef = coef + float(basis[f, j]) * fbuf[step, f]
            part = b_row[j] * coef
            out = part if out is None else out + part
        return out[:, :own], out[:, own:]

    gcol[0:K, :] = off_ref[0] + 1.0
    gcol[K : 2 * K, :] = off_ref[1]
    grow[...] = jnp.zeros_like(grow)
    set_rows(g_re, g_im)
    c_re, c_im = g_re, g_im
    d_re = d_im = jnp.zeros_like(g_re)
    fit_copies = None
    stage = 0
    for admm in range(ADMM):
        for sweep in range(PASSES):
            nr, ni, dn = terms()
            if fit_copies is not None:
                for copy in fit_copies:
                    copy.wait()
                fit_copies = None
                c_re, c_im = fit(admm - 1, None, None)
                d_re = d_re + g_re - c_re
                d_im = d_im + g_im - c_im
            scaling = 1.0 / (dn + pen)
            f_re = (nr + g_re * dn + pen * (c_re - d_re)) * scaling
            f_im = (ni + g_im * dn + pen * (c_im - d_im)) * scaling
            g_re = 0.5 * (g_re + f_re)
            g_im = 0.5 * (g_im + f_im)
            last = admm == ADMM - 1 and sweep == PASSES - 1
            if not last:
                copies = exchange(
                    gbuf, stage, ns, me, "stcol", st_peer, gs_sem, gr_sem,
                    jnp.concatenate([g_re, g_im], axis=1),
                )
            if sweep == PASSES - 1:
                fit_copies = exchange(
                    fbuf, admm, nf, row, "freq", fr_peer, fs_sem, fr_sem,
                    jnp.concatenate([g_re + d_re, g_im + d_im], axis=1),
                )
            if not last:
                set_rows(g_re, g_im)
                for copy in copies:
                    copy.wait()
                gcol[0:K, :] = jnp.concatenate([gbuf[stage, d][:, :own] for d in range(ns)], axis=1)
                gcol[K : 2 * K, :] = jnp.concatenate([gbuf[stage, d][:, own:] for d in range(ns)], axis=1)
                stage += 1
    out_ref[0, 0] = g_re
    out_ref[0, 1] = g_im
    for copy in fit_copies:
        copy.wait()
    c_re, c_im = fit(ADMM - 1, None, None)
    out_ref[1, 0] = c_re
    out_ref[1, 1] = c_im


def hand_out(both_ref, gains_ref, cons_ref):
    gains_ref[...] = both_ref[0]
    cons_ref[...] = both_ref[1]


def on_device(
    visibilities, positions, source_lmn, source_flux, cluster_map, station_order, penalty, offsets
):
    nf = lax.axis_size("freq")
    ns = lax.axis_size("stcol")
    cols = visibilities.shape[2]
    N = visibilities.shape[4]
    K = penalty.shape[0]
    total = source_flux.shape[0]
    S = total // K
    own = N // ns
    assert visibilities.shape[1] == 1 and visibilities.shape[3] == 1
    exchanges = ADMM * PASSES - 1
    vmem = pl.BlockSpec(memory_space=pltpu.VMEM)
    shape = jax.ShapeDtypeStruct((2, K, own), F32)
    dma = pltpu.SemaphoreType.DMA
    both = pl.pallas_call(
        functools.partial(kernel, (nf, ns, K, N, own, cols, S)),
        out_shape=jax.ShapeDtypeStruct((2, 2, K, own), F32),
        in_specs=[vmem] * 8,
        out_specs=vmem,
        scratch_shapes=[
            pltpu.VMEM((ns, cols, 2 * own), F32),
            pltpu.VMEM((ns, cols, 2 * own), F32),
            pltpu.VMEM((S, 128), F32),
            pltpu.VMEM((K, 2 * own, N), F32),
            pltpu.VMEM((2 * own, N), F32),
            pltpu.VMEM((K, 16, N), F32),
            pltpu.VMEM((2 * K, N), F32),
            pltpu.VMEM((own, 128), F32),
            pltpu.VMEM((own, 128), F32),
            pltpu.VMEM((exchanges, ns, K, 2 * own), F32),
            pltpu.VMEM((ADMM, nf, K, 2 * own), F32),
            dma((ns,)),
            dma((ns,)),
            dma((exchanges, ns)),
            dma((exchanges, ns)),
            dma((ADMM, nf)),
            dma((ADMM, nf)),
        ],
        compiler_params=pltpu.CompilerParams(collective_id=0, has_side_effects=True),
        name="calibrate",
    )(
        visibilities.reshape(-1, 128),
        positions,
        source_lmn,
        source_flux.reshape(1, total),
        cluster_map.reshape(1, total),
        station_order.reshape(1, N),
        penalty.reshape(1, K),
        offsets.reshape(2, K, N),
    )
    gains, cons = pl.pallas_call(
        hand_out, out_shape=(shape, shape), in_specs=[vmem], out_specs=(vmem, vmem), name="hand_out"
    )(both)
    return gains[:, None], cons[:, None]


def solution(mesh):
    in_specs = (
        P(None, "freq", "stcol", None, None),
        P(),
        P(),
        P(),
        P(),
        P(),
        P(),
        P(None, "freq", None, None),
    )
    out_specs = (P(None, "freq", None, "stcol"), P(None, "freq", None, "stcol"))
    return jax.shard_map(
        on_device, mesh=mesh, in_specs=in_specs, out_specs=out_specs, check_vma=False
    )
```
